32 devices in a mesh: leaf: 8 (over z, x), sub: 4 (over y, core).
Axes of the slice: x: 2, y: 2, z: 4, core: 2. Of those that a mesh axis runs over, the one named last changes fastest.
Arguments:
- points: bfloat16 [96, 64, 512], P('leaf', None, 'sub'), may hold values from -5 to 5
- charges: bfloat16 [96, 8, 512], P('leaf', None, 'sub'), may hold values from -6 to 6
- near_leaf: int32 [96, 32], P('leaf'), may hold values from -1 to 95, as said below
- far_node: int32 [96, 32], P('leaf'), may hold values from 0 to 31
- skel_index: int32 [32, 256], P(('leaf', 'sub')), may hold values from 0 to 1535, as said below
- skel_weight: bfloat16 [32, 8, 256], P(('leaf', 'sub')), may hold values from -12 to 12
Outputs:
- potential: float32 [96, 8, 512], P('leaf', None, 'sub')
The draws below stay inside these ranges and needn't reach their ends.
Inputs may be any that keep to these rules, and one draw needn't show every extreme that they name: `near_leaf`: entry 0 of the list of leaf l is l itself; every other entry is -1 or a leaf held by another index of leaf. Over the lists of the 12 leaves of one index of leaf no leaf appears twice, and at most 3 distinct leaves of any one other index of leaf appear (leaves k * 12 to k * 12 + 11 belong to index k); every draw reaches 3. `skel_index`: the 256 entries of a row are distinct.
All inputs are finite; a program needn't handle non-finite values.
Results may differ from the reference program's by a relative error of at most 0.0003.
Values may be sent and summed in bfloat16 or wider, within the bound.
A program may use at most 64 MiB of HBM per device.

```python
import jax
import jax.numpy as jnp
from jax import lax

DIM = 64
RHS = 8
P_SIZE = 512
S = 256
NEAR = 32
FAR = 32
CAP = 3
NODE_DEV = 1
LEAF_DEV = 12
SHARES = 4
QUARTER = 128
LEAVES = 96
NODES = 32


def draw_points(key, part):
    values = jax.random.normal(key, (LEAVES, DIM, P_SIZE), jnp.float32)
    return jnp.clip(values, -5.0, 5.0).astype(jnp.bfloat16)


def draw_near_leaf(key, part):
    leaf_count = LEAVES // LEAF_DEV
    lane_ids = jnp.arange(leaf_count, dtype=jnp.int32)
    spots = LEAF_DEV * (NEAR - 1)

    def one_device(target_dev):
        dev_key = jax.random.fold_in(key, target_dev)
        distance = jnp.abs(lane_ids - target_dev)
        distance = jnp.minimum(distance, leaf_count - distance)
        counts = jax.random.randint(jax.random.fold_in(dev_key, 1), (leaf_count,), 1, CAP)
        counts = jnp.where(distance <= 2, CAP, counts)
        counts = jnp.where(distance == 0, 0, counts)
        orders = jax.vmap(lambda source: jax.random.permutation(jax.random.fold_in(dev_key, 100 + source), LEAF_DEV))(lane_ids)
        leaf_ids = lane_ids[:, None] * LEAF_DEV + orders[:, :CAP].astype(jnp.int32)
        is_valid = jnp.arange(CAP)[None, :] < counts[:, None]
        flat_ids = leaf_ids.reshape(-1)
        flat_valid = is_valid.reshape(-1).astype(jnp.int32)
        ranking = jnp.argsort(1 - flat_valid, stable=True)
        pooled = flat_ids[ranking]
        total_valid = jnp.sum(flat_valid)
        position = jnp.arange(spots, dtype=jnp.int32)
        entry_ids = jnp.where(position < total_valid, pooled[jnp.minimum(position, leaf_count * CAP - 1)], -1)
        shuffle = jax.random.permutation(jax.random.fold_in(dev_key, 2), spots)
        entry_ids = entry_ids[shuffle].reshape(LEAF_DEV, NEAR - 1).astype(jnp.int32)
        own_leaves = target_dev * LEAF_DEV + jnp.arange(LEAF_DEV, dtype=jnp.int32)
        return jnp.concatenate([own_leaves[:, None], entry_ids], axis=1)
    return jax.vmap(one_device)(lane_ids).reshape(LEAVES, NEAR)


def draw_skel_index(key, part):
    local_points = LEAF_DEV * QUARTER

    def one_node(node):
        return jax.random.permutation(jax.random.fold_in(key, node), local_points)[:S].astype(jnp.int32)
    return jax.vmap(one_node)(jnp.arange(NODES, dtype=jnp.int32))


def touch_ends(result, stream_key, least, high):
    longest = result.shape.index(max(result.shape))
    spots = []
    for shift in (0, 1):
        where = [jax.random.randint(jax.random.fold_in(stream_key, axis), (), 0, length) for axis, length in enumerate(result.shape)]
        where[longest] = (where[longest] + shift) % result.shape[longest]
        spots.append(tuple(where))
    return result.at[spots[0]].set(least).at[spots[1]].set(high)


def shard_levels(own_key, extent, cuts, least, largest):
    level = 1.0
    for dim, blocks in cuts:
        draws = jax.random.uniform(jax.random.fold_in(jax.random.fold_in(own_key, 6), dim), (blocks,), jnp.float32, least / len(cuts), largest / len(cuts))
        level = level * jnp.repeat(jnp.exp(draws), extent[dim] // blocks).reshape((-1,) + (1,) * (len(extent) - 1 - dim))
    return level


def centred(key, shape, width, bound, cuts=(), kind=jnp.bfloat16):
    entries = width * jax.random.normal(key, shape, jnp.float32)
    if cuts:
        entries = entries * shard_levels(key, shape, cuts, -0.22, 0.18)
    return jnp.clip(entries, -bound, bound).astype(kind)


def setup_inputs(seed: int = 0) -> dict:
    splits = jax.random.split(jax.random.key(seed), 7)
    points = draw_points(jax.random.fold_in(splits[6], 71), 0)
    charges = centred(splits[1], (LEAVES, RHS, P_SIZE), 1.0, 6.0, ((0, 8), (2, 4)))
    near_leaf = draw_near_leaf(jax.random.fold_in(splits[6], 71), 0)
    far_node = touch_ends(jax.random.randint(splits[3], (LEAVES, FAR), 0, NODES), jax.random.fold_in(splits[3], 1), 0, NODES - 1).astype(jnp.int32)
    skel_index = draw_skel_index(jax.random.fold_in(splits[6], 71), 0)
    skel_weight = centred(splits[5], (NODES, RHS, S), 2.0, 12.0, ((0, 32),))
    return dict(points=points, charges=charges, near_leaf=near_leaf, far_node=far_node, skel_index=skel_index, skel_weight=skel_weight)


RATE_SCALE = 2.5


def kernel_apply(targets, sources, weights, alive):
    target_wide = targets.astype(jnp.float32)
    source_wide = sources.astype(jnp.float32)
    target_sq = jnp.sum(target_wide * target_wide, axis=0)
    source_sq = jnp.sum(source_wide * source_wide, axis=1)
    inner_prod = jnp.einsum('dr,mdc->rmc', target_wide, source_wide, precision=lax.Precision.HIGHEST)
    distance = target_sq[:, None, None] + source_sq[None] - 2.0 * inner_prod
    decay_rate = RATE_SCALE / targets.shape[0]
    kernel_block = jnp.exp(-decay_rate * distance)
    masked = weights.astype(jnp.float32) * alive[:, None, None]
    return jnp.einsum('rmc,mkc->kr', kernel_block, masked, precision=lax.Precision.HIGHEST)


def reference(points, charges, near_leaf, far_node, skel_index, skel_weight):
    def near_one(pieces):
        target, entry_list = pieces
        alive = entry_list >= 0
        clamped = jnp.where(alive, entry_list, 0)
        return kernel_apply(target, points[clamped], charges[clamped], alive.astype(jnp.float32))

    near_term = lax.map(near_one, (points, near_leaf))
    node_total = skel_index.shape[0]
    owner_dev = jnp.arange(node_total, dtype=jnp.int32) // NODE_DEV
    base_leaf = (owner_dev // SHARES) * LEAF_DEV
    base_column = (owner_dev % SHARES) * QUARTER
    leaf_pos = base_leaf[:, None] + skel_index // QUARTER
    column_pos = base_column[:, None] + skel_index % QUARTER
    skeleton_points = jnp.swapaxes(points[leaf_pos, :, column_pos], 1, 2)

    def far_one(pieces):
        target, node_list = pieces
        alive = jnp.ones(node_list.shape, jnp.float32)
        return kernel_apply(target, skeleton_points[node_list], skel_weight[node_list], alive)

    far_term = lax.map(far_one, (points, far_node))
    return near_term + far_term
```

```python
import functools
import math

import jax
import jax.numpy as jnp
from jax import lax
from jax.experimental import pallas as pl
from jax.experimental.pallas import tpu as pltpu
from jax.sharding import PartitionSpec as P

CAP = 3
RATE_SCALE = 2.5
ROWS = 80


def split3(x):
    a = x.astype(jnp.bfloat16).astype(jnp.float32)
    b = (x - a).astype(jnp.bfloat16).astype(jnp.float32)
    return a, b, (x - a) - b


def stack_rows(main, first, second):
    rows, width = 16, main.shape[1]
    row_id = lax.broadcasted_iota(jnp.int32, (rows, width), 0)
    extra = jnp.zeros((rows, width), jnp.float32)
    for k, piece in enumerate(tuple(first) + tuple(second)):
        extra = jnp.where(row_id == k, piece, extra)
    pad = jnp.zeros((128 - rows - main.shape[0], width), jnp.float32)
    return jnp.concatenate([main, extra, pad], axis=0)


def compute_kernel(
    owner_ref, count_ref, own_ref, charge_ref, tgt_ref, near_ref, skel_ref, out_ref,
    taug, ysrc, yskel, acc, list_ref
):
    leaf_dev, features, quarter = own_ref.shape
    shares = tgt_ref.shape[0]
    slots = near_ref.shape[0]
    nodes = skel_ref.shape[0]
    skel_size = skel_ref.shape[2]
    coef = -(RATE_SCALE / features) * math.log2(math.e)
    one = jnp.ones((1, 1), jnp.float32)

    def source_rows(block):
        wide = block.astype(jnp.float32)
        sq = split3(jnp.sum(wide * wide, axis=0, keepdims=True))
        return stack_rows(wide, (one, one, one), sq)

    def prep(l, carry):
        for q in range(shares):
            wide = tgt_ref[q, l].astype(jnp.float32)
            sq = split3(jnp.sum(wide * wide, axis=0, keepdims=True))
            taug[l, :, q * quarter : (q + 1) * quarter] = stack_rows(
                -2.0 * wide, sq, (one, one, one)
            ).astype(jnp.bfloat16)
        ysrc[l] = source_rows(own_ref[l]).T.astype(jnp.bfloat16)
        return carry

    lax.fori_loop(0, leaf_dev, prep, 0)

    def prep_near(b, carry):
        ysrc[leaf_dev + b] = source_rows(near_ref[b, :features]).T.astype(jnp.bfloat16)
        return carry

    lax.fori_loop(0, slots, prep_near, 0)

    def prep_skel(n, carry):
        for h in range(skel_size // 128):
            block = skel_ref[n, :features, h * 128 : (h + 1) * 128]
            yskel[n, h * 128 : (h + 1) * 128] = source_rows(block).T.astype(jnp.bfloat16)
        return carry

    lax.fori_loop(0, nodes, prep_skel, 0)

    def item(l, sources, weights):
        parts = []
        half = 2 * quarter
        for h in range(shares * quarter // half):
            dist = jnp.dot(
                sources, taug[l, :, h * half : (h + 1) * half],
                preferred_element_type=jnp.float32,
            )
            kern = jnp.exp2(coef * dist)
            high = kern.astype(jnp.bfloat16)
            low = (kern - high.astype(jnp.float32)).astype(jnp.bfloat16)
            parts.append(
                jnp.dot(weights, high, preferred_element_type=jnp.float32)
                + jnp.dot(weights, low, preferred_element_type=jnp.float32)
            )
        return jnp.concatenate(parts, axis=1)

    def own_step(l, carry):
        acc[l] = item(l, ysrc[l], charge_ref[l])
        return carry

    lax.fori_loop(0, leaf_dev, own_step, 0)

    def scan_near(b, pos):
        list_ref[pos] = b
        return pos + (owner_ref[b] >= 0).astype(jnp.int32)

    live = lax.fori_loop(0, slots, scan_near, 0)

    def near_step(i, carry):
        b = list_ref[i]
        l = owner_ref[b]
        acc[l] += item(l, ysrc[leaf_dev + b], near_ref[b, features : features + 8])
        return carry

    lax.fori_loop(0, live, near_step, 0)

    def scan_far(p, pos):
        list_ref[pos] = p
        return pos + (count_ref[p] > 0).astype(jnp.int32)

    pairs = lax.fori_loop(0, leaf_dev * nodes, scan_far, 0)

    def far_step(i, carry):
        p = list_ref[i]
        l = p // nodes
        n = p - l * nodes
        value = item(l, yskel[n], skel_ref[n, features : features + 8])
        acc[l] += value * count_ref[p].astype(jnp.float32)
        return carry

    lax.fori_loop(0, pairs, far_step, 0)

    for q in range(shares):
        out_ref[q] = acc[:, :, q * quarter : (q + 1) * quarter]


def compute(owner, count, points, charges, targets, near, skel):
    leaf_dev, features, quarter = points.shape
    shares = targets.shape[0]
    slots, nodes, skel_size = near.shape[0], skel.shape[0], skel.shape[2]
    vmem = pl.BlockSpec(memory_space=pltpu.VMEM)
    smem = pl.BlockSpec(memory_space=pltpu.SMEM)
    return pl.pallas_call(
        compute_kernel,
        out_shape=jax.ShapeDtypeStruct((shares, leaf_dev, 8, quarter), jnp.float32),
        in_specs=[smem, smem] + [vmem] * 5,
        out_specs=vmem,
        scratch_shapes=[
            pltpu.VMEM((leaf_dev, 128, shares * quarter), jnp.bfloat16),
            pltpu.VMEM((leaf_dev + slots, quarter, 128), jnp.bfloat16),
            pltpu.VMEM((nodes, skel_size, 128), jnp.bfloat16),
            pltpu.VMEM((leaf_dev, 8, shares * quarter), jnp.float32),
            pltpu.SMEM((max(leaf_dev * nodes, slots) + 1,), jnp.int32),
        ],
        compiler_params=pltpu.CompilerParams(vmem_limit_bytes=56 * 1024 * 1024),
    )(owner, count, points, charges, targets, near, skel)


def plan(near_leaf, far_node, node_dev, leaf_count, shares):
    leaf_dev = near_leaf.shape[0]
    own_index = lax.axis_index("leaf")
    all_ids = jnp.arange(leaf_count * leaf_dev, dtype=jnp.int32)
    leaf_ids = jnp.arange(leaf_dev, dtype=jnp.int32)
    marks = jnp.where(near_leaf[:, :, None] == all_ids, leaf_ids[:, None, None] + 1, 0)
    wanted_by = jnp.max(marks, axis=(0, 1)).reshape(leaf_count, leaf_dev)
    other = jnp.arange(leaf_count, dtype=jnp.int32)[:, None] != own_index
    wanted_by = jnp.where(other, wanted_by, 0)
    want = wanted_by > 0
    before = leaf_ids[:, None] > leaf_ids[None, :]
    rank = jnp.sum(jnp.where(before[None] & want[:, None, :], 1, 0), axis=2)
    slot_ids = jnp.arange(CAP, dtype=jnp.int32)
    hit = want[:, None, :] & (rank[:, None, :] == slot_ids[None, :, None])
    owner = jnp.max(jnp.where(hit, wanted_by[:, None, :], 0), axis=2) - 1
    leaf_of_slot = jnp.max(jnp.where(hit, leaf_ids, 0), axis=2)
    ids = jnp.arange(leaf_count, dtype=jnp.int32) * shares + lax.axis_index("sub")
    ids = (ids[:, None] * node_dev + jnp.arange(node_dev, dtype=jnp.int32)).reshape(-1)
    count = jnp.sum((far_node[:, :, None] == ids).astype(jnp.int32), axis=1)
    return owner.reshape(-1), leaf_of_slot, count.reshape(-1)


def shards(points, charges, near_leaf, far_node, skel_index, skel_weight):
    leaf_dev, features, quarter = points.shape
    leaf_count, shares = lax.axis_size("leaf"), lax.axis_size("sub")
    node_dev, skel_size = skel_index.shape
    owner, leaf_of_slot, count = plan(near_leaf, far_node, node_dev, leaf_count, shares)
    asked = lax.all_to_all(leaf_of_slot, "leaf", split_axis=0, concat_axis=0, tiled=True)
    both = jnp.concatenate(
        [points, charges, jnp.zeros((leaf_dev, ROWS - features - 8, quarter), points.dtype)], axis=1
    )
    send = both[asked.reshape(-1)].reshape(leaf_count, CAP, ROWS, quarter)
    near = lax.all_to_all(send, "leaf", split_axis=0, concat_axis=0, tiled=True)
    near = near.reshape(leaf_count * CAP, ROWS, quarter)
    targets = lax.all_gather(points, "sub", axis=0, tiled=False)
    flat = jnp.transpose(points, (1, 0, 2)).reshape(features, leaf_dev * quarter)
    picked = jnp.take(flat, skel_index.reshape(-1), axis=1)
    picked = jnp.transpose(picked.reshape(features, node_dev, skel_size), (1, 0, 2))
    block = jnp.concatenate(
        [picked, skel_weight, jnp.zeros((node_dev, ROWS - features - 8, skel_size), points.dtype)],
        axis=1,
    )
    skel = lax.all_gather(block, "leaf", axis=0, tiled=True)
    partial = compute(owner, count, points, charges, targets, near, skel)
    return lax.psum_scatter(partial, "sub", scatter_dimension=0, tiled=False)


def solution(mesh):
    in_specs = (
        P("leaf", None, "sub"),
        P("leaf", None, "sub"),
        P("leaf", None),
        P("leaf", None),
        P(("leaf", "sub"), None),
        P(("leaf", "sub"), None, None),
    )
    out_specs = P("leaf", None, "sub")
    return jax.shard_map(shards, mesh=mesh, in_specs=in_specs, out_specs=out_specs, check_vma=False)
```

```python
import functools
import math

import jax
import jax.numpy as jnp
from jax import lax
from jax.experimental import pallas as pl
from jax.experimental.pallas import tpu as pltpu
from jax.sharding import PartitionSpec as P

CAP = 3
RATE_SCALE = 2.5
ROWS = 80
MESH = pl.DeviceIdType.MESH


def split3(x):
    a = x.astype(jnp.bfloat16).astype(jnp.float32)
    b = (x - a).astype(jnp.bfloat16).astype(jnp.float32)
    return a, b, (x - a) - b


def stack_rows(main, first, second):
    rows, width = 16, main.shape[1]
    row_id = lax.broadcasted_iota(jnp.int32, (rows, width), 0)
    extra = jnp.zeros((rows, width), jnp.float32)
    for k, piece in enumerate(tuple(first) + tuple(second)):
        extra = jnp.where(row_id == k, piece, extra)
    pad = jnp.zeros((128 - rows - main.shape[0], width), jnp.float32)
    return jnp.concatenate([main, extra, pad], axis=0)


def compute_kernel(
    owner_ref, count_ref, own_ref, charge_ref, tgt_ref, near_ref, skel_ref, out_ref,
    taug, ysrc, yskel, acc, list_ref
):
    leaf_dev, features, quarter = own_ref.shape
    shares = tgt_ref.shape[0]
    slots = near_ref.shape[0]
    nodes = skel_ref.shape[0]
    skel_size = skel_ref.shape[2]
    coef = -(RATE_SCALE / features) * math.log2(math.e)
    one = jnp.ones((1, 1), jnp.float32)

    def source_rows(block):
        wide = block.astype(jnp.float32)
        sq = split3(jnp.sum(wide * wide, axis=0, keepdims=True))
        return stack_rows(wide, (one, one, one), sq)

    def prep(l, carry):
        for q in range(shares):
            wide = tgt_ref[q, l].astype(jnp.float32)
            sq = split3(jnp.sum(wide * wide, axis=0, keepdims=True))
            taug[l, :, q * quarter : (q + 1) * quarter] = stack_rows(
                -2.0 * wide, sq, (one, one, one)
            ).astype(jnp.bfloat16)
        ysrc[l] = source_rows(own_ref[l]).T.astype(jnp.bfloat16)
        return carry

    lax.fori_loop(0, leaf_dev, prep, 0)

    def prep_near(b, carry):
        ysrc[leaf_dev + b] = source_rows(near_ref[b, :features]).T.astype(jnp.bfloat16)
        return carry

    lax.fori_loop(0, slots, prep_near, 0)

    def prep_skel(n, carry):
        for h in range(skel_size // 128):
            block = skel_ref[n, :features, h * 128 : (h + 1) * 128]
            yskel[n, h * 128 : (h + 1) * 128] = source_rows(block).T.astype(jnp.bfloat16)
        return carry

    lax.fori_loop(0, nodes, prep_skel, 0)

    def item(l, sources, weights):
        parts = []
        half = 2 * quarter
        for h in range(shares * quarter // half):
            dist = jnp.dot(
                sources, taug[l, :, h * half : (h + 1) * half],
                preferred_element_type=jnp.float32,
            )
            kern = jnp.exp2(coef * dist)
            high = kern.astype(jnp.bfloat16)
            low = (kern - high.astype(jnp.float32)).astype(jnp.bfloat16)
            parts.append(
                jnp.dot(weights, high, preferred_element_type=jnp.float32)
                + jnp.dot(weights, low, preferred_element_type=jnp.float32)
            )
        return jnp.concatenate(parts, axis=1)

    def own_step(l, carry):
        acc[l] = item(l, ysrc[l], charge_ref[l])
        return carry

    lax.fori_loop(0, leaf_dev, own_step, 0)

    def scan_near(b, pos):
        list_ref[pos] = b
        return pos + (owner_ref[b] >= 0).astype(jnp.int32)

    live = lax.fori_loop(0, slots, scan_near, 0)

    def near_step(i, carry):
        b = list_ref[i]
        l = owner_ref[b]
        acc[l] += item(l, ysrc[leaf_dev + b], near_ref[b, features : features + 8])
        return carry

    lax.fori_loop(0, live, near_step, 0)

    def scan_far(p, pos):
        list_ref[pos] = p
        return pos + (count_ref[p] > 0).astype(jnp.int32)

    pairs = lax.fori_loop(0, leaf_dev * nodes, scan_far, 0)

    def far_step(i, carry):
        p = list_ref[i]
        l = p // nodes
        n = p - l * nodes
        value = item(l, yskel[n], skel_ref[n, features : features + 8])
        acc[l] += value * count_ref[p].astype(jnp.float32)
        return carry

    lax.fori_loop(0, pairs, far_step, 0)

    for q in range(shares):
        out_ref[q] = acc[:, :, q * quarter : (q + 1) * quarter]


def compute(owner, count, points, charges, targets, near, skel):
    leaf_dev, features, quarter = points.shape
    shares = targets.shape[0]
    slots, nodes, skel_size = near.shape[0], skel.shape[0], skel.shape[2]
    vmem = pl.BlockSpec(memory_space=pltpu.VMEM)
    smem = pl.BlockSpec(memory_space=pltpu.SMEM)
    return pl.pallas_call(
        compute_kernel,
        out_shape=jax.ShapeDtypeStruct((shares, leaf_dev, 8, quarter), jnp.float32),
        in_specs=[smem, smem] + [vmem] * 5,
        out_specs=vmem,
        scratch_shapes=[
            pltpu.VMEM((leaf_dev, 128, shares * quarter), jnp.bfloat16),
            pltpu.VMEM((leaf_dev + slots, quarter, 128), jnp.bfloat16),
            pltpu.VMEM((nodes, skel_size, 128), jnp.bfloat16),
            pltpu.VMEM((leaf_dev, 8, shares * quarter), jnp.float32),
            pltpu.SMEM((max(leaf_dev * nodes, slots) + 1,), jnp.int32),
        ],
        compiler_params=pltpu.CompilerParams(vmem_limit_bytes=56 * 1024 * 1024),
    )(owner, count, points, charges, targets, near, skel)


def exchange_kernel(
    leaf_count, shares, points_ref, charge_ref, ask_ref, index_ref, weight_ref,
    tgt_ref, near_ref, skel_ref,
    wide, send_buf, asked, tgt_send, tgt_recv, ask_send, ask_recv, near_send, near_recv,
    skel_send, skel_recv, local_sem
):
    leaf_dev, features, quarter = points_ref.shape
    node_dev, skel_size = index_ref.shape
    me = lax.axis_index("leaf")
    part = lax.axis_index("sub")

    barrier = pltpu.get_barrier_semaphore()

    def greet_leaf(o, carry):
        pl.semaphore_signal(
            barrier, inc=1, device_id={"leaf": lax.rem(me + o, leaf_count)}, device_id_type=MESH
        )
        return carry

    def greet_sub(o, carry):
        pl.semaphore_signal(
            barrier, inc=1, device_id={"sub": lax.rem(part + o, shares)}, device_id_type=MESH
        )
        return carry

    lax.fori_loop(1, leaf_count, greet_leaf, 0)
    lax.fori_loop(1, shares, greet_sub, 0)
    pl.semaphore_wait(barrier, leaf_count + shares - 2)

    def target_copy(o):
        return pltpu.make_async_remote_copy(
            src_ref=points_ref, dst_ref=tgt_ref.at[part],
            send_sem=tgt_send.at[o], recv_sem=tgt_recv.at[o],
            device_id={"sub": lax.rem(part + o, shares)}, device_id_type=MESH,
        )

    def ask_copy(o):
        k = lax.rem(me + o, leaf_count)
        return pltpu.make_async_remote_copy(
            src_ref=ask_ref.at[k], dst_ref=asked.at[o],
            send_sem=ask_send.at[o], recv_sem=ask_recv.at[o],
            device_id={"leaf": k}, device_id_type=MESH,
        )

    def near_copy(o):
        return pltpu.make_async_remote_copy(
            src_ref=send_buf.at[o], dst_ref=near_ref.at[me],
            send_sem=near_send.at[o], recv_sem=near_recv.at[o],
            device_id={"leaf": lax.rem(me + leaf_count - o, leaf_count)}, device_id_type=MESH,
        )

    def skel_copy(o):
        return pltpu.make_async_remote_copy(
            src_ref=skel_ref.at[me], dst_ref=skel_ref.at[me],
            send_sem=skel_send.at[o], recv_sem=skel_recv.at[o],
            device_id={"leaf": lax.rem(me + o, leaf_count)}, device_id_type=MESH,
        )

    def run(low, high, act):
        def step(o, carry):
            act(o)
            return carry

        lax.fori_loop(low, high, step, 0)

    run(1, leaf_count, lambda o: ask_copy(o).start())
    run(1, shares, lambda o: target_copy(o).start())
    own = pltpu.make_async_copy(points_ref, tgt_ref.at[part], local_sem)
    own.start()

    for i in range(node_dev):
        index = index_ref[i : i + 1, :]
        picked = jnp.zeros((features, skel_size), jnp.float32)
        spot = lax.broadcasted_iota(jnp.int32, (quarter, skel_size), 0)
        for j in range(leaf_dev):
            pick = jnp.where(spot + j * quarter == index, 1.0, 0.0).astype(jnp.bfloat16)
            picked += jnp.dot(points_ref[j], pick, preferred_element_type=jnp.float32)
        skel_ref[me, i] = jnp.concatenate(
            [picked, weight_ref[i].astype(jnp.float32),
             jnp.zeros((ROWS - features - 8, skel_size), jnp.float32)], axis=0
        ).astype(jnp.bfloat16)
    run(1, leaf_count, lambda o: skel_copy(o).start())

    for j in range(leaf_dev):
        wide[j] = jnp.concatenate(
            [points_ref[j].astype(jnp.float32), charge_ref[j].astype(jnp.float32),
             jnp.zeros((ROWS - features - 8, quarter), jnp.float32)], axis=0
        )

    def pack(o):
        ask_copy(o).wait_recv()
        for c in range(CAP):
            row = asked[o, c : c + 1, :]
            block = wide[0]
            for j in range(1, leaf_dev):
                block = jnp.where(row == j, wide[j], block)
            send_buf[o, c] = block.astype(jnp.bfloat16)
        near_copy(o).start()

    run(1, leaf_count, pack)
    own.wait()
    run(1, leaf_count, lambda o: ask_copy(o).wait_send())
    run(1, shares, lambda o: target_copy(o).wait())
    run(1, leaf_count, lambda o: skel_copy(o).wait())
    run(1, leaf_count, lambda o: near_copy(o).wait())


def exchange(points, charges, ask, skel_index, skel_weight, leaf_count, shares):
    leaf_dev, features, quarter = points.shape
    node_dev, skel_size = skel_index.shape
    vmem = pl.BlockSpec(memory_space=pltpu.VMEM)
    dma = pltpu.SemaphoreType.DMA
    return pl.pallas_call(
        functools.partial(exchange_kernel, leaf_count, shares),
        out_shape=(
            jax.ShapeDtypeStruct((shares, leaf_dev, features, quarter), jnp.bfloat16),
            jax.ShapeDtypeStruct((leaf_count, CAP, ROWS, quarter), jnp.bfloat16),
            jax.ShapeDtypeStruct((leaf_count, node_dev, ROWS, skel_size), jnp.bfloat16),
        ),
        in_specs=[vmem] * 5,
        out_specs=(vmem, vmem, vmem),
        scratch_shapes=[
            pltpu.VMEM((leaf_dev, ROWS, quarter), jnp.float32),
            pltpu.VMEM((leaf_count, CAP, ROWS, quarter), jnp.bfloat16),
            pltpu.VMEM((leaf_count, 8, 128), jnp.int32),
            dma((shares,)), dma((shares,)),
            dma((leaf_count,)), dma((leaf_count,)),
            dma((leaf_count,)), dma((leaf_count,)),
            dma((leaf_count,)), dma((leaf_count,)),
            dma,
        ],
        compiler_params=pltpu.CompilerParams(
            collective_id=0, has_side_effects=True, vmem_limit_bytes=56 * 1024 * 1024
        ),
    )(points, charges, ask, skel_index, skel_weight)


def reduce_kernel(shares, partial_ref, out_ref, held, send_sem, recv_sem):
    part = lax.axis_index("sub")
    barrier = pltpu.get_barrier_semaphore()
    for o in range(1, shares):
        pl.semaphore_signal(
            barrier, inc=1, device_id={"sub": lax.rem(part + o, shares)}, device_id_type=MESH
        )
    pl.semaphore_wait(barrier, shares - 1)
    copies = []
    for o in range(1, shares):
        other = lax.rem(part + o, shares)
        copy = pltpu.make_async_remote_copy(
            src_ref=partial_ref.at[other], dst_ref=held.at[o],
            send_sem=send_sem.at[o], recv_sem=recv_sem.at[o],
            device_id={"sub": other}, device_id_type=MESH,
        )
        copy.start()
        copies.append(copy)
    for copy in copies:
        copy.wait()
    total = partial_ref[part]
    for o in range(1, shares):
        total += held[o]
    out_ref[...] = total


def reduce_parts(partial):
    shares = partial.shape[0]
    vmem = pl.BlockSpec(memory_space=pltpu.VMEM)
    return pl.pallas_call(
        functools.partial(reduce_kernel, shares),
        out_shape=jax.ShapeDtypeStruct(partial.shape[1:], jnp.float32),
        in_specs=[vmem],
        out_specs=vmem,
        scratch_shapes=[
            pltpu.VMEM(partial.shape, jnp.float32),
            pltpu.SemaphoreType.DMA((shares,)),
            pltpu.SemaphoreType.DMA((shares,)),
        ],
        compiler_params=pltpu.CompilerParams(collective_id=1, has_side_effects=True),
    )(partial)


def plan(near_leaf, far_node, node_dev, leaf_count, shares):
    leaf_dev = near_leaf.shape[0]
    own_index = lax.axis_index("leaf")
    all_ids = jnp.arange(leaf_count * leaf_dev, dtype=jnp.int32)
    leaf_ids = jnp.arange(leaf_dev, dtype=jnp.int32)
    marks = jnp.where(near_leaf[:, :, None] == all_ids, leaf_ids[:, None, None] + 1, 0)
    wanted_by = jnp.max(marks, axis=(0, 1)).reshape(leaf_count, leaf_dev)
    other = jnp.arange(leaf_count, dtype=jnp.int32)[:, None] != own_index
    wanted_by = jnp.where(other, wanted_by, 0)
    want = wanted_by > 0
    before = leaf_ids[:, None] > leaf_ids[None, :]
    rank = jnp.sum(jnp.where(before[None] & want[:, None, :], 1, 0), axis=2)
    slot_ids = jnp.arange(CAP, dtype=jnp.int32)
    hit = want[:, None, :] & (rank[:, None, :] == slot_ids[None, :, None])
    owner = jnp.max(jnp.where(hit, wanted_by[:, None, :], 0), axis=2) - 1
    leaf_of_slot = jnp.max(jnp.where(hit, leaf_ids, 0), axis=2)
    ids = jnp.arange(leaf_count, dtype=jnp.int32) * shares + lax.axis_index("sub")
    ids = (ids[:, None] * node_dev + jnp.arange(node_dev, dtype=jnp.int32)).reshape(-1)
    count = jnp.sum((far_node[:, :, None] == ids).astype(jnp.int32), axis=1)
    return owner.reshape(-1), leaf_of_slot, count.reshape(-1)


def shards(points, charges, near_leaf, far_node, skel_index, skel_weight):
    leaf_dev, features, quarter = points.shape
    leaf_count, shares = lax.axis_size("leaf"), lax.axis_size("sub")
    node_dev, skel_size = skel_index.shape
    owner, leaf_of_slot, count = plan(near_leaf, far_node, node_dev, leaf_count, shares)
    ask = jnp.pad(leaf_of_slot, ((0, 0), (0, 8 - CAP)))
    ask = jnp.broadcast_to(ask[:, :, None], (leaf_count, 8, 128))
    targets, near, skel = exchange(
        points, charges, ask, skel_index, skel_weight, leaf_count, shares
    )
    near = near.reshape(leaf_count * CAP, ROWS, quarter)
    skel = skel.reshape(leaf_count * node_dev, ROWS, skel_size)
    partial = compute(owner, count, points, charges, targets, near, skel)
    return reduce_parts(partial)


def solution(mesh):
    in_specs = (
        P("leaf", None, "sub"),
        P("leaf", None, "sub"),
        P("leaf", None),
        P("leaf", None),
        P(("leaf", "sub"), None),
        P(("leaf", "sub"), None, None),
    )
    out_specs = P("leaf", None, "sub")
    return jax.shard_map(shards, mesh=mesh, in_specs=in_specs, out_specs=out_specs, check_vma=False)
```

```python
import functools
import math

import jax
import jax.numpy as jnp
from jax import lax
from jax.experimental import pallas as pl
from jax.experimental.pallas import tpu as pltpu
from jax.sharding import PartitionSpec as P

CAP = 3
RATE_SCALE = 2.5
ROWS = 80
FAR_UNROLL = 8
NEAR_UNROLL = 4
PREP = 4
MESH = pl.DeviceIdType.MESH


def split3(x):
    a = x.astype(jnp.bfloat16).astype(jnp.float32)
    b = (x - a).astype(jnp.bfloat16).astype(jnp.float32)
    return a, b, (x - a) - b


def stack_rows(main, first, second):
    rows, width = 16, main.shape[1]
    row_id = lax.broadcasted_iota(jnp.int32, (rows, width), 0)
    extra = jnp.zeros((rows, width), jnp.float32)
    for k, piece in enumerate(tuple(first) + tuple(second)):
        extra = jnp.where(row_id == k, piece, extra)
    pad = jnp.zeros((128 - rows - main.shape[0], width), jnp.float32)
    return jnp.concatenate([main, extra, pad], axis=0)


def compute_kernel(
    owner_ref, count_ref, own_ref, charge_ref, tgt_ref, near_ref, skel_ref, out_ref,
    taug, ysrc, yskel, acc, list_ref
):
    leaf_dev, features, quarter = own_ref.shape
    shares = tgt_ref.shape[0]
    slots = near_ref.shape[0]
    nodes = skel_ref.shape[0]
    skel_size = skel_ref.shape[2]
    coef = -(RATE_SCALE / features) * math.log2(math.e)
    one = jnp.ones((1, 1), jnp.float32)

    def source_rows(block):
        wide = block.astype(jnp.float32)
        sq = split3(jnp.sum(wide * wide, axis=0, keepdims=True))
        return stack_rows(wide, (one, one, one), sq)

    def prep(l, carry):
        for q in range(shares):
            wide = tgt_ref[q, l].astype(jnp.float32)
            sq = split3(jnp.sum(wide * wide, axis=0, keepdims=True))
            taug[l, :, q * quarter : (q + 1) * quarter] = stack_rows(
                -2.0 * wide, sq, (one, one, one)
            ).astype(jnp.bfloat16)
        ysrc[l] = source_rows(own_ref[l]).T.astype(jnp.bfloat16)
        return carry

    lax.fori_loop(0, leaf_dev, prep, 0, unroll=PREP)

    def prep_near(b, carry):
        ysrc[leaf_dev + b] = source_rows(near_ref[b, :features]).T.astype(jnp.bfloat16)
        return carry

    lax.fori_loop(0, slots, prep_near, 0, unroll=PREP)

    def prep_skel(n, carry):
        for h in range(skel_size // 128):
            block = skel_ref[n, :features, h * 128 : (h + 1) * 128]
            yskel[n, h * 128 : (h + 1) * 128] = source_rows(block).T.astype(jnp.bfloat16)
        return carry

    lax.fori_loop(0, nodes, prep_skel, 0, unroll=PREP)

    def item(l, sources, weights):
        parts = []
        half = 2 * quarter
        for h in range(shares * quarter // half):
            dist = jnp.dot(
                sources, taug[l, :, h * half : (h + 1) * half],
                preferred_element_type=jnp.float32,
            )
            kern = jnp.exp2(coef * dist)
            high = kern.astype(jnp.bfloat16)
            low = (kern - high.astype(jnp.float32)).astype(jnp.bfloat16)
            parts.append(
                jnp.dot(weights, high, preferred_element_type=jnp.float32)
                + jnp.dot(weights, low, preferred_element_type=jnp.float32)
            )
        return jnp.concatenate(parts, axis=1)

    def own_step(l, carry):
        acc[l] = item(l, ysrc[l], charge_ref[l])
        return carry

    lax.fori_loop(0, leaf_dev, own_step, 0, unroll=NEAR_UNROLL)

    def scan_near(b, pos):
        list_ref[pos] = b
        return pos + (owner_ref[b] >= 0).astype(jnp.int32)

    live = lax.fori_loop(0, slots, scan_near, 0)
    for u in range(NEAR_UNROLL - 1):
        list_ref[live + u] = 0

    def near_step(i, carry):
        found = []
        for u in range(NEAR_UNROLL):
            b = list_ref[i * NEAR_UNROLL + u]
            l = jnp.maximum(owner_ref[b], 0)
            value = item(l, ysrc[leaf_dev + b], near_ref[b, features : features + 8])
            found.append((l, jnp.where(i * NEAR_UNROLL + u < live, value, 0.0)))
        for l, value in found:
            acc[l] += value
        return carry

    lax.fori_loop(0, (live + NEAR_UNROLL - 1) // NEAR_UNROLL, near_step, 0)

    def scan_far(p, pos):
        list_ref[pos] = p
        return pos + (count_ref[p] > 0).astype(jnp.int32)

    pairs = lax.fori_loop(0, leaf_dev * nodes, scan_far, 0)
    for u in range(FAR_UNROLL - 1):
        list_ref[pairs + u] = 0

    def far_step(i, carry):
        found = []
        for u in range(FAR_UNROLL):
            p = list_ref[i * FAR_UNROLL + u]
            l = p // nodes
            n = p - l * nodes
            value = item(l, yskel[n], skel_ref[n, features : features + 8])
            times = jnp.where(i * FAR_UNROLL + u < pairs, count_ref[p], 0)
            found.append((l, value * times.astype(jnp.float32)))
        for l, value in found:
            acc[l] += value
        return carry

    lax.fori_loop(0, (pairs + FAR_UNROLL - 1) // FAR_UNROLL, far_step, 0)

    for q in range(shares):
        out_ref[q] = acc[:, :, q * quarter : (q + 1) * quarter]


def compute(owner, count, points, charges, targets, near, skel):
    leaf_dev, features, quarter = points.shape
    shares = targets.shape[0]
    slots, nodes, skel_size = near.shape[0], skel.shape[0], skel.shape[2]
    vmem = pl.BlockSpec(memory_space=pltpu.VMEM)
    smem = pl.BlockSpec(memory_space=pltpu.SMEM)
    return pl.pallas_call(
        compute_kernel,
        out_shape=jax.ShapeDtypeStruct((shares, leaf_dev, 8, quarter), jnp.float32),
        in_specs=[smem, smem] + [vmem] * 5,
        out_specs=vmem,
        scratch_shapes=[
            pltpu.VMEM((leaf_dev, 128, shares * quarter), jnp.bfloat16),
            pltpu.VMEM((leaf_dev + slots, quarter, 128), jnp.bfloat16),
            pltpu.VMEM((nodes, skel_size, 128), jnp.bfloat16),
            pltpu.VMEM((leaf_dev, 8, shares * quarter), jnp.float32),
            pltpu.SMEM((max(leaf_dev * nodes, slots) + FAR_UNROLL,), jnp.int32),
        ],
        compiler_params=pltpu.CompilerParams(vmem_limit_bytes=56 * 1024 * 1024),
    )(owner, count, points, charges, targets, near, skel)


def exchange_kernel(
    leaf_count, shares, points_ref, charge_ref, ask_ref, index_ref, weight_ref,
    tgt_ref, near_ref, skel_ref,
    wide, send_buf, asked, tgt_send, tgt_recv, ask_send, ask_recv, near_send, near_recv,
    skel_send, skel_recv, local_sem
):
    leaf_dev, features, quarter = points_ref.shape
    node_dev, skel_size = index_ref.shape
    me = lax.axis_index("leaf")
    part = lax.axis_index("sub")

    barrier = pltpu.get_barrier_semaphore()

    def greet_leaf(o, carry):
        pl.semaphore_signal(
            barrier, inc=1, device_id={"leaf": lax.rem(me + o, leaf_count)}, device_id_type=MESH
        )
        return carry

    def greet_sub(o, carry):
        pl.semaphore_signal(
            barrier, inc=1, device_id={"sub": lax.rem(part + o, shares)}, device_id_type=MESH
        )
        return carry

    lax.fori_loop(1, leaf_count, greet_leaf, 0)
    lax.fori_loop(1, shares, greet_sub, 0)
    pl.semaphore_wait(barrier, leaf_count + shares - 2)

    def target_copy(o):
        return pltpu.make_async_remote_copy(
            src_ref=points_ref, dst_ref=tgt_ref.at[part],
            send_sem=tgt_send.at[o], recv_sem=tgt_recv.at[o],
            device_id={"sub": lax.rem(part + o, shares)}, device_id_type=MESH,
        )

    def ask_copy(o):
        k = lax.rem(me + o, leaf_count)
        return pltpu.make_async_remote_copy(
            src_ref=ask_ref.at[k], dst_ref=asked.at[o],
            send_sem=ask_send.at[o], recv_sem=ask_recv.at[o],
            device_id={"leaf": k}, device_id_type=MESH,
        )

    def near_copy(o):
        return pltpu.make_async_remote_copy(
            src_ref=send_buf.at[o], dst_ref=near_ref.at[me],
            send_sem=near_send.at[o], recv_sem=near_recv.at[o],
            device_id={"leaf": lax.rem(me + leaf_count - o, leaf_count)}, device_id_type=MESH,
        )

    def skel_copy(o):
        return pltpu.make_async_remote_copy(
            src_ref=skel_ref.at[me], dst_ref=skel_ref.at[me],
            send_sem=skel_send.at[o], recv_sem=skel_recv.at[o],
            device_id={"leaf": lax.rem(me + o, leaf_count)}, device_id_type=MESH,
        )

    def run(low, high, act):
        def step(o, carry):
            act(o)
            return carry

        lax.fori_loop(low, high, step, 0)

    run(1, leaf_count, lambda o: ask_copy(o).start())
    run(1, shares, lambda o: target_copy(o).start())
    own = pltpu.make_async_copy(points_ref, tgt_ref.at[part], local_sem)
    own.start()

    for i in range(node_dev):
        index = index_ref[i : i + 1, :]
        picked = jnp.zeros((features, skel_size), jnp.float32)
        spot = lax.broadcasted_iota(jnp.int32, (quarter, skel_size), 0)
        for j in range(leaf_dev):
            pick = jnp.where(spot + j * quarter == index, 1.0, 0.0).astype(jnp.bfloat16)
            picked += jnp.dot(points_ref[j], pick, preferred_element_type=jnp.float32)
        skel_ref[me, i] = jnp.concatenate(
            [picked, weight_ref[i].astype(jnp.float32),
             jnp.zeros((ROWS - features - 8, skel_size), jnp.float32)], axis=0
        ).astype(jnp.bfloat16)
    run(1, leaf_count, lambda o: skel_copy(o).start())

    for j in range(leaf_dev):
        wide[j] = jnp.concatenate(
            [points_ref[j].astype(jnp.float32), charge_ref[j].astype(jnp.float32),
             jnp.zeros((ROWS - features - 8, quarter), jnp.float32)], axis=0
        )

    def pack(o):
        ask_copy(o).wait_recv()
        for c in range(CAP):
            row = asked[o, c : c + 1, :]
            block = wide[0]
            for j in range(1, leaf_dev):
                block = jnp.where(row == j, wide[j], block)
            send_buf[o, c] = block.astype(jnp.bfloat16)
        near_copy(o).start()

    run(1, leaf_count, pack)
    own.wait()
    run(1, leaf_count, lambda o: ask_copy(o).wait_send())
    run(1, shares, lambda o: target_copy(o).wait())
    run(1, leaf_count, lambda o: skel_copy(o).wait())
    run(1, leaf_count, lambda o: near_copy(o).wait())


def exchange(points, charges, ask, skel_index, skel_weight, leaf_count, shares):
    leaf_dev, features, quarter = points.shape
    node_dev, skel_size = skel_index.shape
    vmem = pl.BlockSpec(memory_space=pltpu.VMEM)
    dma = pltpu.SemaphoreType.DMA
    return pl.pallas_call(
        functools.partial(exchange_kernel, leaf_count, shares),
        out_shape=(
            jax.ShapeDtypeStruct((shares, leaf_dev, features, quarter), jnp.bfloat16),
            jax.ShapeDtypeStruct((leaf_count, CAP, ROWS, quarter), jnp.bfloat16),
            jax.ShapeDtypeStruct((leaf_count, node_dev, ROWS, skel_size), jnp.bfloat16),
        ),
        in_specs=[vmem] * 5,
        out_specs=(vmem, vmem, vmem),
        scratch_shapes=[
            pltpu.VMEM((leaf_dev, ROWS, quarter), jnp.float32),
            pltpu.VMEM((leaf_count, CAP, ROWS, quarter), jnp.bfloat16),
            pltpu.VMEM((leaf_count, 8, 128), jnp.int32),
            dma((shares,)), dma((shares,)),
            dma((leaf_count,)), dma((leaf_count,)),
            dma((leaf_count,)), dma((leaf_count,)),
            dma((leaf_count,)), dma((leaf_count,)),
            dma,
        ],
        compiler_params=pltpu.CompilerParams(
            collective_id=0, has_side_effects=True, vmem_limit_bytes=56 * 1024 * 1024
        ),
    )(points, charges, ask, skel_index, skel_weight)


def reduce_kernel(shares, partial_ref, out_ref, held, send_sem, recv_sem):
    part = lax.axis_index("sub")
    barrier = pltpu.get_barrier_semaphore()
    for o in range(1, shares):
        pl.semaphore_signal(
            barrier, inc=1, device_id={"sub": lax.rem(part + o, shares)}, device_id_type=MESH
        )
    pl.semaphore_wait(barrier, shares - 1)
    copies = []
    for o in range(1, shares):
        other = lax.rem(part + o, shares)
        copy = pltpu.make_async_remote_copy(
            src_ref=partial_ref.at[other], dst_ref=held.at[o],
            send_sem=send_sem.at[o], recv_sem=recv_sem.at[o],
            device_id={"sub": other}, device_id_type=MESH,
        )
        copy.start()
        copies.append(copy)
    for copy in copies:
        copy.wait()
    total = partial_ref[part]
    for o in range(1, shares):
        total += held[o]
    out_ref[...] = total


def reduce_parts(partial):
    shares = partial.shape[0]
    vmem = pl.BlockSpec(memory_space=pltpu.VMEM)
    return pl.pallas_call(
        functools.partial(reduce_kernel, shares),
        out_shape=jax.ShapeDtypeStruct(partial.shape[1:], jnp.float32),
        in_specs=[vmem],
        out_specs=vmem,
        scratch_shapes=[
            pltpu.VMEM(partial.shape, jnp.float32),
            pltpu.SemaphoreType.DMA((shares,)),
            pltpu.SemaphoreType.DMA((shares,)),
        ],
        compiler_params=pltpu.CompilerParams(collective_id=1, has_side_effects=True),
    )(partial)


def plan(near_leaf, far_node, node_dev, leaf_count, shares):
    leaf_dev = near_leaf.shape[0]
    own_index = lax.axis_index("leaf")
    all_ids = jnp.arange(leaf_count * leaf_dev, dtype=jnp.int32)
    leaf_ids = jnp.arange(leaf_dev, dtype=jnp.int32)
    marks = jnp.where(near_leaf[:, :, None] == all_ids, leaf_ids[:, None, None] + 1, 0)
    wanted_by = jnp.max(marks, axis=(0, 1)).reshape(leaf_count, leaf_dev)
    other = jnp.arange(leaf_count, dtype=jnp.int32)[:, None] != own_index
    wanted_by = jnp.where(other, wanted_by, 0)
    want = wanted_by > 0
    before = leaf_ids[:, None] > leaf_ids[None, :]
    rank = jnp.sum(jnp.where(before[None] & want[:, None, :], 1, 0), axis=2)
    slot_ids = jnp.arange(CAP, dtype=jnp.int32)
    hit = want[:, None, :] & (rank[:, None, :] == slot_ids[None, :, None])
    owner = jnp.max(jnp.where(hit, wanted_by[:, None, :], 0), axis=2) - 1
    leaf_of_slot = jnp.max(jnp.where(hit, leaf_ids, 0), axis=2)
    ids = jnp.arange(leaf_count, dtype=jnp.int32) * shares + lax.axis_index("sub")
    ids = (ids[:, None] * node_dev + jnp.arange(node_dev, dtype=jnp.int32)).reshape(-1)
    count = jnp.sum((far_node[:, :, None] == ids).astype(jnp.int32), axis=1)
    return owner.reshape(-1), leaf_of_slot, count.reshape(-1)


def shards(points, charges, near_leaf, far_node, skel_index, skel_weight):
    leaf_dev, features, quarter = points.shape
    leaf_count, shares = lax.axis_size("leaf"), lax.axis_size("sub")
    node_dev, skel_size = skel_index.shape
    owner, leaf_of_slot, count = plan(near_leaf, far_node, node_dev, leaf_count, shares)
    ask = jnp.pad(leaf_of_slot, ((0, 0), (0, 8 - CAP)))
    ask = jnp.broadcast_to(ask[:, :, None], (leaf_count, 8, 128))
    targets, near, skel = exchange(
        points, charges, ask, skel_index, skel_weight, leaf_count, shares
    )
    near = near.reshape(leaf_count * CAP, ROWS, quarter)
    skel = skel.reshape(leaf_count * node_dev, ROWS, skel_size)
    partial = compute(owner, count, points, charges, targets, near, skel)
    return reduce_parts(partial)


def solution(mesh):
    in_specs = (
        P("leaf", None, "sub"),
        P("leaf", None, "sub"),
        P("leaf", None),
        P("leaf", None),
        P(("leaf", "sub"), None),
        P(("leaf", "sub"), None, None),
    )
    out_specs = P("leaf", None, "sub")
    return jax.shard_map(shards, mesh=mesh, in_specs=in_specs, out_specs=out_specs, check_vma=False)
```

```python
import functools
import math

import jax
import jax.numpy as jnp
from jax import lax
from jax.experimental import pallas as pl
from jax.experimental.pallas import tpu as pltpu
from jax.sharding import PartitionSpec as P

CAP = 3
RATE_SCALE = 2.5
ROWS = 80
PREP = 4
NEAR_UNROLL = 4
SLOT_UNROLL = 7
MESH = pl.DeviceIdType.MESH


def split3(x):
    a = x.astype(jnp.bfloat16).astype(jnp.float32)
    b = (x - a).astype(jnp.bfloat16).astype(jnp.float32)
    return a, b, (x - a) - b


def stack_rows(main, first, second):
    rows, width = 16, main.shape[1]
    row_id = lax.broadcasted_iota(jnp.int32, (rows, width), 0)
    extra = jnp.zeros((rows, width), jnp.float32)
    for k, piece in enumerate(tuple(first) + tuple(second)):
        extra = jnp.where(row_id == k, piece, extra)
    pad = jnp.zeros((128 - rows - main.shape[0], width), jnp.float32)
    return jnp.concatenate([main, extra, pad], axis=0)


def fused_kernel(
    leaf_count, shares, owner_ref, count_ref, points_ref, charge_ref, ask_ref, index_ref,
    weight_ref, out_ref, tgt_ref, near_ref, skel_ref, wide, send_buf, asked, taug, yown, ynear,
    yskel, acc, stage, held, tgt_send, tgt_recv, ask_send, ask_recv, near_send, near_recv,
    skel_send, skel_recv, sum_send, sum_recv
):
    leaf_dev, features, quarter = points_ref.shape
    node_dev, skel_size = index_ref.shape
    nodes = leaf_count * node_dev
    coef = -(RATE_SCALE / features) * math.log2(math.e)
    one = jnp.ones((1, 1), jnp.float32)
    me = lax.axis_index("leaf")
    part = lax.axis_index("sub")

    barrier = pltpu.get_barrier_semaphore()

    def greet_leaf(o, carry):
        pl.semaphore_signal(
            barrier, inc=1, device_id={"leaf": lax.rem(me + o, leaf_count)}, device_id_type=MESH
        )
        return carry

    def greet_sub(o, carry):
        pl.semaphore_signal(
            barrier, inc=1, device_id={"sub": lax.rem(part + o, shares)}, device_id_type=MESH
        )
        return carry

    lax.fori_loop(1, leaf_count, greet_leaf, 0)
    lax.fori_loop(1, shares, greet_sub, 0)
    pl.semaphore_wait(barrier, leaf_count + shares - 2)

    def target_copy(o):
        return pltpu.make_async_remote_copy(
            src_ref=points_ref, dst_ref=tgt_ref.at[o],
            send_sem=tgt_send.at[o], recv_sem=tgt_recv.at[o],
            device_id={"sub": lax.rem(part + o, shares)}, device_id_type=MESH,
        )

    def ask_copy(o):
        k = lax.rem(me + o, leaf_count)
        return pltpu.make_async_remote_copy(
            src_ref=ask_ref.at[k], dst_ref=asked.at[o],
            send_sem=ask_send.at[o], recv_sem=ask_recv.at[o],
            device_id={"leaf": k}, device_id_type=MESH,
        )

    def near_copy(o):
        return pltpu.make_async_remote_copy(
            src_ref=send_buf.at[o], dst_ref=near_ref.at[me],
            send_sem=near_send.at[o], recv_sem=near_recv.at[o],
            device_id={"leaf": lax.rem(me + leaf_count - o, leaf_count)}, device_id_type=MESH,
        )

    def skel_copy(o):
        return pltpu.make_async_remote_copy(
            src_ref=skel_ref.at[me], dst_ref=skel_ref.at[me],
            send_sem=skel_send.at[o], recv_sem=skel_recv.at[o],
            device_id={"leaf": lax.rem(me + o, leaf_count)}, device_id_type=MESH,
        )

    def run(low, high, act):
        def step(o, carry):
            act(o)
            return carry

        lax.fori_loop(low, high, step, 0)

    run(1, leaf_count, lambda o: ask_copy(o).start())
    run(1, shares, lambda o: target_copy(o).start())
    for i in range(node_dev):
        index = index_ref[i : i + 1, :]
        picked = jnp.zeros((features, skel_size), jnp.float32)
        spot = lax.broadcasted_iota(jnp.int32, (quarter, skel_size), 0)
        for j in range(leaf_dev):
            pick = jnp.where(spot + j * quarter == index, 1.0, 0.0).astype(jnp.bfloat16)
            picked += jnp.dot(points_ref[j], pick, preferred_element_type=jnp.float32)
        skel_ref[me, i] = jnp.concatenate(
            [picked, weight_ref[i].astype(jnp.float32),
             jnp.zeros((ROWS - features - 8, skel_size), jnp.float32)], axis=0
        ).astype(jnp.bfloat16)
    run(1, leaf_count, lambda o: skel_copy(o).start())

    for j in range(leaf_dev):
        wide[j] = jnp.concatenate(
            [points_ref[j].astype(jnp.float32), charge_ref[j].astype(jnp.float32),
             jnp.zeros((ROWS - features - 8, quarter), jnp.float32)], axis=0
        )


    def pack(o):
        ask_copy(o).wait_recv()
        for c in range(CAP):
            row = asked[o, c : c + 1, :]
            block = wide[0]
            for j in range(1, leaf_dev):
                block = jnp.where(row == j, wide[j], block)
            send_buf[o, c] = block.astype(jnp.bfloat16)
        near_copy(o).start()

    run(1, leaf_count, pack)

    def source_rows(block):
        rows = block.astype(jnp.float32)
        sq = split3(jnp.sum(rows * rows, axis=0, keepdims=True))
        return stack_rows(rows, (one, one, one), sq)

    def prep_targets(o, l, block):
        rows = block.astype(jnp.float32)
        sq = split3(jnp.sum(rows * rows, axis=0, keepdims=True))
        taug[l, :, o * quarter : (o + 1) * quarter] = stack_rows(
            -2.0 * rows, sq, (one, one, one)
        ).astype(jnp.bfloat16)

    def prep_own(l, carry):
        yown[l] = source_rows(points_ref[l]).T.astype(jnp.bfloat16)
        prep_targets(0, l, points_ref[l])
        return carry

    lax.fori_loop(0, leaf_dev, prep_own, 0, unroll=PREP)

    for o in range(1, shares):
        target_copy(o).wait_recv()

    def prep_rest(l, carry):
        for o in range(1, shares):
            prep_targets(o, l, tgt_ref[o, l])
        return carry

    lax.fori_loop(0, leaf_dev, prep_rest, 0, unroll=PREP)

    def item(l, sources, weights):
        parts = []
        half = 2 * quarter
        for h in range(shares * quarter // half):
            dist = jnp.dot(
                sources, taug[l, :, h * half : (h + 1) * half],
                preferred_element_type=jnp.float32,
            )
            kern = jnp.exp2(coef * dist)
            high = kern.astype(jnp.bfloat16)
            low = (kern - high.astype(jnp.float32)).astype(jnp.bfloat16)
            parts.append(
                jnp.dot(weights, high, preferred_element_type=jnp.float32)
                + jnp.dot(weights, low, preferred_element_type=jnp.float32)
            )
        return jnp.concatenate(parts, axis=1)

    def own_step(l, carry):
        acc[l] = item(l, yown[l], charge_ref[l])
        return carry

    lax.fori_loop(0, leaf_dev, own_step, 0, unroll=NEAR_UNROLL)

    def far_step(o, carry):
        @pl.when(o > 0)
        def _():
            skel_copy(o).wait_recv()

        k = lax.rem(me + leaf_count - o, leaf_count)
        for i in range(node_dev):
            for h in range(skel_size // 128):
                block = skel_ref[k, i, :features, h * 128 : (h + 1) * 128]
                yskel[h * 128 : (h + 1) * 128] = source_rows(block).T.astype(jnp.bfloat16)
            weights = skel_ref[k, i, features : features + 8]
            for l in range(leaf_dev):
                times = count_ref[l * nodes + k * node_dev + i].astype(jnp.float32)
                acc[l] += times * item(l, yskel[...], weights)
        return carry

    lax.fori_loop(0, leaf_count, far_step, 0)

    run(1, leaf_count, lambda o: near_copy(o).wait_recv())

    def prep_near(o, carry):
        k = lax.rem(me + o, leaf_count)
        for c in range(CAP):
            ynear[o, c] = source_rows(near_ref[k, c, :features]).T.astype(jnp.bfloat16)
        return carry

    lax.fori_loop(1, leaf_count, prep_near, 0)

    def near_step(o, carry):
        k = lax.rem(me + o, leaf_count)
        found = []
        for c in range(CAP):
            owner = owner_ref[k * CAP + c]
            value = item(
                jnp.maximum(owner, 0), ynear[o, c], near_ref[k, c, features : features + 8]
            )
            found.append((owner, value))
        for l in range(leaf_dev):
            add = jnp.zeros_like(found[0][1])
            for owner, value in found:
                add += jnp.where(owner == l, value, 0.0)
            acc[l] += add
        return carry

    lax.fori_loop(1, leaf_count, near_step, 0, unroll=SLOT_UNROLL)

    def sum_copy(o):
        return pltpu.make_async_remote_copy(
            src_ref=stage.at[o], dst_ref=held.at[o],
            send_sem=sum_send.at[o], recv_sem=sum_recv.at[o],
            device_id={"sub": lax.rem(part + shares - o, shares)}, device_id_type=MESH,
        )

    for o in range(1, shares):
        stage[o] = acc[:, :, o * quarter : (o + 1) * quarter]
        sum_copy(o).start()
    run(1, leaf_count, lambda o: ask_copy(o).wait_send())
    run(1, shares, lambda o: target_copy(o).wait_send())
    run(1, leaf_count, lambda o: skel_copy(o).wait_send())
    run(1, leaf_count, lambda o: near_copy(o).wait_send())
    total = acc[:, :, :quarter]
    for o in range(1, shares):
        sum_copy(o).wait_recv()
        total += held[o]
    out_ref[...] = total
    for o in range(1, shares):
        sum_copy(o).wait_send()


def fused(owner, count, points, charges, ask, skel_index, skel_weight, leaf_count, shares):
    leaf_dev, features, quarter = points.shape
    node_dev, skel_size = skel_index.shape
    vmem = pl.BlockSpec(memory_space=pltpu.VMEM)
    smem = pl.BlockSpec(memory_space=pltpu.SMEM)
    dma = pltpu.SemaphoreType.DMA
    bf16, f32 = jnp.bfloat16, jnp.float32
    return pl.pallas_call(
        functools.partial(fused_kernel, leaf_count, shares),
        out_shape=jax.ShapeDtypeStruct((leaf_dev, 8, quarter), f32),
        in_specs=[smem, smem] + [vmem] * 5,
        out_specs=vmem,
        scratch_shapes=[
            pltpu.VMEM((shares, leaf_dev, features, quarter), bf16),
            pltpu.VMEM((leaf_count, CAP, ROWS, quarter), bf16),
            pltpu.VMEM((leaf_count, node_dev, ROWS, skel_size), bf16),
            pltpu.VMEM((leaf_dev, ROWS, quarter), f32),
            pltpu.VMEM((leaf_count, CAP, ROWS, quarter), bf16),
            pltpu.VMEM((leaf_count, 8, 128), jnp.int32),
            pltpu.VMEM((leaf_dev, 128, shares * quarter), bf16),
            pltpu.VMEM((leaf_dev, quarter, 128), bf16),
            pltpu.VMEM((leaf_count, CAP, quarter, 128), bf16),
            pltpu.VMEM((skel_size, 128), bf16),
            pltpu.VMEM((leaf_dev, 8, shares * quarter), f32),
            pltpu.VMEM((shares, leaf_dev, 8, quarter), f32),
            pltpu.VMEM((shares, leaf_dev, 8, quarter), f32),
            dma((shares,)), dma((shares,)),
            dma((leaf_count,)), dma((leaf_count,)),
            dma((leaf_count,)), dma((leaf_count,)),
            dma((leaf_count,)), dma((leaf_count,)),
            dma((shares,)), dma((shares,)),
        ],
        compiler_params=pltpu.CompilerParams(
            collective_id=0, has_side_effects=True, vmem_limit_bytes=56 * 1024 * 1024
        ),
    )(owner, count, points, charges, ask, skel_index, skel_weight)


def plan(near_leaf, far_node, node_dev, leaf_count, shares):
    leaf_dev = near_leaf.shape[0]
    own_index = lax.axis_index("leaf")
    all_ids = jnp.arange(leaf_count * leaf_dev, dtype=jnp.int32)
    leaf_ids = jnp.arange(leaf_dev, dtype=jnp.int32)
    marks = jnp.where(near_leaf[:, :, None] == all_ids, leaf_ids[:, None, None] + 1, 0)
    wanted_by = jnp.max(marks, axis=(0, 1)).reshape(leaf_count, leaf_dev)
    other = jnp.arange(leaf_count, dtype=jnp.int32)[:, None] != own_index
    wanted_by = jnp.where(other, wanted_by, 0)
    want = wanted_by > 0
    before = leaf_ids[:, None] > leaf_ids[None, :]
    rank = jnp.sum(jnp.where(before[None] & want[:, None, :], 1, 0), axis=2)
    slot_ids = jnp.arange(CAP, dtype=jnp.int32)
    hit = want[:, None, :] & (rank[:, None, :] == slot_ids[None, :, None])
    owner = jnp.max(jnp.where(hit, wanted_by[:, None, :], 0), axis=2) - 1
    leaf_of_slot = jnp.max(jnp.where(hit, leaf_ids, 0), axis=2)
    ids = jnp.arange(leaf_count, dtype=jnp.int32) * shares + lax.axis_index("sub")
    ids = (ids[:, None] * node_dev + jnp.arange(node_dev, dtype=jnp.int32)).reshape(-1)
    count = jnp.sum((far_node[:, :, None] == ids).astype(jnp.int32), axis=1)
    return owner.reshape(-1), leaf_of_slot, count.reshape(-1)


def shards(points, charges, near_leaf, far_node, skel_index, skel_weight):
    leaf_count, shares = lax.axis_size("leaf"), lax.axis_size("sub")
    node_dev = skel_index.shape[0]
    owner, leaf_of_slot, count = plan(near_leaf, far_node, node_dev, leaf_count, shares)
    ask = jnp.pad(leaf_of_slot, ((0, 0), (0, 8 - CAP)))
    ask = jnp.broadcast_to(ask[:, :, None], (leaf_count, 8, 128))
    return fused(
        owner, count, points, charges, ask, skel_index, skel_weight, leaf_count, shares
    )


def solution(mesh):
    in_specs = (
        P("leaf", None, "sub"),
        P("leaf", None, "sub"),
        P("leaf", None),
        P("leaf", None),
        P(("leaf", "sub"), None),
        P(("leaf", "sub"), None, None),
    )
    out_specs = P("leaf", None, "sub")
    return jax.shard_map(shards, mesh=mesh, in_specs=in_specs, out_specs=out_specs, check_vma=False)
```

```python
import functools
import math

import jax
import jax.numpy as jnp
from jax import lax
from jax.experimental import pallas as pl
from jax.experimental.pallas import tpu as pltpu
from jax.sharding import PartitionSpec as P

CAP = 3
RATE_SCALE = 2.5
ROWS = 80
PREP = 4
NEAR_UNROLL = 4
SLOT_UNROLL = 7
MESH = pl.DeviceIdType.MESH


def split3(x):
    a = x.astype(jnp.bfloat16).astype(jnp.float32)
    b = (x - a).astype(jnp.bfloat16).astype(jnp.float32)
    return a, b, (x - a) - b


def stack_rows(main, first, second):
    rows, width = 16, main.shape[1]
    row_id = lax.broadcasted_iota(jnp.int32, (rows, width), 0)
    extra = jnp.zeros((rows, width), jnp.float32)
    for k, piece in enumerate(tuple(first) + tuple(second)):
        extra = jnp.where(row_id == k, piece, extra)
    pad = jnp.zeros((128 - rows - main.shape[0], width), jnp.float32)
    return jnp.concatenate([main, extra, pad], axis=0)


def fused_kernel(
    leaf_count, shares, owner_ref, count_ref, slot_ref, points_ref, charge_ref, index_ref,
    weight_ref, out_ref, ask_ref, tgt_ref, near_ref, skel_ref, wide, send_buf, asked, taug, yown, ynear,
    yskel, acc, stage, held, tgt_send, tgt_recv, ask_send, ask_recv, near_send, near_recv,
    skel_send, skel_recv, sum_send, sum_recv
):
    leaf_dev, features, quarter = points_ref.shape
    node_dev, skel_size = index_ref.shape
    coef = -(RATE_SCALE / features) * math.log2(math.e)
    one = jnp.ones((1, 1), jnp.float32)
    me = lax.axis_index("leaf")
    part = lax.axis_index("sub")

    barrier = pltpu.get_barrier_semaphore()

    def greet_leaf(o, carry):
        pl.semaphore_signal(
            barrier, inc=1, device_id={"leaf": lax.rem(me + o, leaf_count)}, device_id_type=MESH
        )
        return carry

    def greet_sub(o, carry):
        pl.semaphore_signal(
            barrier, inc=1, device_id={"sub": lax.rem(part + o, shares)}, device_id_type=MESH
        )
        return carry

    def fill_ask(k, carry):
        for c in range(CAP):
            ask_ref[k, c : c + 1, :] = jnp.full((1, 128), slot_ref[k, c], jnp.int32)
        ask_ref[k, CAP:, :] = jnp.zeros((8 - CAP, 128), jnp.int32)
        return carry

    lax.fori_loop(1, leaf_count, greet_leaf, 0)
    lax.fori_loop(1, shares, greet_sub, 0)
    lax.fori_loop(0, leaf_count, fill_ask, 0)
    pl.semaphore_wait(barrier, leaf_count + shares - 2)

    def target_copy(o):
        return pltpu.make_async_remote_copy(
            src_ref=points_ref, dst_ref=tgt_ref.at[o],
            send_sem=tgt_send.at[o], recv_sem=tgt_recv.at[o],
            device_id={"sub": lax.rem(part + o, shares)}, device_id_type=MESH,
        )

    def ask_copy(o):
        k = lax.rem(me + o, leaf_count)
        return pltpu.make_async_remote_copy(
            src_ref=ask_ref.at[k], dst_ref=asked.at[o],
            send_sem=ask_send.at[o], recv_sem=ask_recv.at[o],
            device_id={"leaf": k}, device_id_type=MESH,
        )

    def near_copy(o):
        return pltpu.make_async_remote_copy(
            src_ref=send_buf.at[o], dst_ref=near_ref.at[me],
            send_sem=near_send.at[o], recv_sem=near_recv.at[o],
            device_id={"leaf": lax.rem(me + leaf_count - o, leaf_count)}, device_id_type=MESH,
        )

    def skel_copy(o):
        return pltpu.make_async_remote_copy(
            src_ref=skel_ref.at[me], dst_ref=skel_ref.at[me],
            send_sem=skel_send.at[o], recv_sem=skel_recv.at[o],
            device_id={"leaf": lax.rem(me + o, leaf_count)}, device_id_type=MESH,
        )

    def run(low, high, act):
        def step(o, carry):
            act(o)
            return carry

        lax.fori_loop(low, high, step, 0)

    run(1, leaf_count, lambda o: ask_copy(o).start())
    run(1, shares, lambda o: target_copy(o).start())
    for i in range(node_dev):
        index = index_ref[i : i + 1, :]
        picked = jnp.zeros((features, skel_size), jnp.float32)
        spot = lax.broadcasted_iota(jnp.int32, (quarter, skel_size), 0)
        for j in range(leaf_dev):
            pick = jnp.where(spot + j * quarter == index, 1.0, 0.0).astype(jnp.bfloat16)
            picked += jnp.dot(points_ref[j], pick, preferred_element_type=jnp.float32)
        skel_ref[me, i] = jnp.concatenate(
            [picked, weight_ref[i].astype(jnp.float32),
             jnp.zeros((ROWS - features - 8, skel_size), jnp.float32)], axis=0
        ).astype(jnp.bfloat16)
    run(1, leaf_count, lambda o: skel_copy(o).start())

    for j in range(leaf_dev):
        wide[j] = jnp.concatenate(
            [points_ref[j].astype(jnp.float32), charge_ref[j].astype(jnp.float32),
             jnp.zeros((ROWS - features - 8, quarter), jnp.float32)], axis=0
        )


    def pack(o):
        ask_copy(o).wait_recv()
        for c in range(CAP):
            row = asked[o, c : c + 1, :]
            block = wide[0]
            for j in range(1, leaf_dev):
                block = jnp.where(row == j, wide[j], block)
            send_buf[o, c] = block.astype(jnp.bfloat16)
        near_copy(o).start()

    run(1, leaf_count, pack)

    def source_rows(block):
        rows = block.astype(jnp.float32)
        sq = split3(jnp.sum(rows * rows, axis=0, keepdims=True))
        return stack_rows(rows, (one, one, one), sq)

    def prep_targets(o, l, block):
        rows = block.astype(jnp.float32)
        sq = split3(jnp.sum(rows * rows, axis=0, keepdims=True))
        taug[l, :, o * quarter : (o + 1) * quarter] = stack_rows(
            -2.0 * rows, sq, (one, one, one)
        ).astype(jnp.bfloat16)

    def prep_own(l, carry):
        yown[l] = source_rows(points_ref[l]).T.astype(jnp.bfloat16)
        prep_targets(0, l, points_ref[l])
        return carry

    lax.fori_loop(0, leaf_dev, prep_own, 0, unroll=PREP)

    for o in range(1, shares):
        target_copy(o).wait_recv()

    def prep_rest(l, carry):
        for o in range(1, shares):
            prep_targets(o, l, tgt_ref[o, l])
        return carry

    lax.fori_loop(0, leaf_dev, prep_rest, 0, unroll=PREP)

    def item(l, sources, weights):
        parts = []
        half = 2 * quarter
        for h in range(shares * quarter // half):
            dist = jnp.dot(
                sources, taug[l, :, h * half : (h + 1) * half],
                preferred_element_type=jnp.float32,
            )
            kern = jnp.exp2(coef * dist)
            high = kern.astype(jnp.bfloat16)
            low = (kern - high.astype(jnp.float32)).astype(jnp.bfloat16)
            parts.append(
                jnp.dot(weights, high, preferred_element_type=jnp.float32)
                + jnp.dot(weights, low, preferred_element_type=jnp.float32)
            )
        return jnp.concatenate(parts, axis=1)

    def own_step(l, carry):
        acc[l] = item(l, yown[l], charge_ref[l])
        return carry

    lax.fori_loop(0, leaf_dev, own_step, 0, unroll=NEAR_UNROLL)

    def far_step(o, carry):
        @pl.when(o > 0)
        def _():
            skel_copy(o).wait_recv()

        k = lax.rem(me + leaf_count - o, leaf_count)
        for i in range(node_dev):
            for h in range(skel_size // 128):
                block = skel_ref[k, i, :features, h * 128 : (h + 1) * 128]
                yskel[h * 128 : (h + 1) * 128] = source_rows(block).T.astype(jnp.bfloat16)
            weights = skel_ref[k, i, features : features + 8]
            for l in range(leaf_dev):
                times = count_ref[l, k * node_dev + i].astype(jnp.float32)
                acc[l] += times * item(l, yskel[...], weights)
        return carry

    lax.fori_loop(0, leaf_count, far_step, 0)

    run(1, leaf_count, lambda o: near_copy(o).wait_recv())

    def prep_near(o, carry):
        k = lax.rem(me + o, leaf_count)
        for c in range(CAP):
            ynear[o, c] = source_rows(near_ref[k, c, :features]).T.astype(jnp.bfloat16)
        return carry

    lax.fori_loop(1, leaf_count, prep_near, 0)

    def near_step(o, carry):
        k = lax.rem(me + o, leaf_count)
        found = []
        for c in range(CAP):
            owner = owner_ref[k, c]
            value = item(
                jnp.maximum(owner, 0), ynear[o, c], near_ref[k, c, features : features + 8]
            )
            found.append((owner, value))
        for l in range(leaf_dev):
            add = jnp.zeros_like(found[0][1])
            for owner, value in found:
                add += jnp.where(owner == l, value, 0.0)
            acc[l] += add
        return carry

    lax.fori_loop(1, leaf_count, near_step, 0, unroll=SLOT_UNROLL)

    def sum_copy(o):
        return pltpu.make_async_remote_copy(
            src_ref=stage.at[o], dst_ref=held.at[o],
            send_sem=sum_send.at[o], recv_sem=sum_recv.at[o],
            device_id={"sub": lax.rem(part + shares - o, shares)}, device_id_type=MESH,
        )

    for o in range(1, shares):
        stage[o] = acc[:, :, o * quarter : (o + 1) * quarter]
        sum_copy(o).start()
    run(1, leaf_count, lambda o: ask_copy(o).wait_send())
    run(1, shares, lambda o: target_copy(o).wait_send())
    run(1, leaf_count, lambda o: skel_copy(o).wait_send())
    run(1, leaf_count, lambda o: near_copy(o).wait_send())
    total = acc[:, :, :quarter]
    for o in range(1, shares):
        sum_copy(o).wait_recv()
        total += held[o]
    out_ref[...] = total
    for o in range(1, shares):
        sum_copy(o).wait_send()


def fused(owner, count, slot_leaf, points, charges, skel_index, skel_weight, leaf_count, shares):
    leaf_dev, features, quarter = points.shape
    node_dev, skel_size = skel_index.shape
    vmem = pl.BlockSpec(memory_space=pltpu.VMEM)
    smem = pl.BlockSpec(memory_space=pltpu.SMEM)
    dma = pltpu.SemaphoreType.DMA
    bf16, f32 = jnp.bfloat16, jnp.float32
    return pl.pallas_call(
        functools.partial(fused_kernel, leaf_count, shares),
        out_shape=jax.ShapeDtypeStruct((leaf_dev, 8, quarter), f32),
        in_specs=[smem] * 3 + [vmem] * 4,
        out_specs=vmem,
        scratch_shapes=[
            pltpu.VMEM((leaf_count, 8, 128), jnp.int32),
            pltpu.VMEM((shares, leaf_dev, features, quarter), bf16),
            pltpu.VMEM((leaf_count, CAP, ROWS, quarter), bf16),
            pltpu.VMEM((leaf_count, node_dev, ROWS, skel_size), bf16),
            pltpu.VMEM((leaf_dev, ROWS, quarter), f32),
            pltpu.VMEM((leaf_count, CAP, ROWS, quarter), bf16),
            pltpu.VMEM((leaf_count, 8, 128), jnp.int32),
            pltpu.VMEM((leaf_dev, 128, shares * quarter), bf16),
            pltpu.VMEM((leaf_dev, quarter, 128), bf16),
            pltpu.VMEM((leaf_count, CAP, quarter, 128), bf16),
            pltpu.VMEM((skel_size, 128), bf16),
            pltpu.VMEM((leaf_dev, 8, shares * quarter), f32),
            pltpu.VMEM((shares, leaf_dev, 8, quarter), f32),
            pltpu.VMEM((shares, leaf_dev, 8, quarter), f32),
            dma((shares,)), dma((shares,)),
            dma((leaf_count,)), dma((leaf_count,)),
            dma((leaf_count,)), dma((leaf_count,)),
            dma((leaf_count,)), dma((leaf_count,)),
            dma((shares,)), dma((shares,)),
        ],
        compiler_params=pltpu.CompilerParams(
            collective_id=0, has_side_effects=True, vmem_limit_bytes=56 * 1024 * 1024
        ),
    )(owner, count, slot_leaf, points, charges, skel_index, skel_weight)


def plan(near_leaf, far_node, node_dev, leaf_count, shares):
    leaf_dev = near_leaf.shape[0]
    own_index = lax.axis_index("leaf")
    all_ids = jnp.arange(leaf_count * leaf_dev, dtype=jnp.int32)
    leaf_ids = jnp.arange(leaf_dev, dtype=jnp.int32)
    marks = jnp.where(near_leaf[:, :, None] == all_ids, leaf_ids[:, None, None] + 1, 0)
    wanted_by = jnp.max(marks, axis=(0, 1)).reshape(leaf_count, leaf_dev)
    other = jnp.arange(leaf_count, dtype=jnp.int32)[:, None] != own_index
    wanted_by = jnp.where(other, wanted_by, 0)
    want = wanted_by > 0
    before = leaf_ids[:, None] > leaf_ids[None, :]
    rank = jnp.sum(jnp.where(before[None] & want[:, None, :], 1, 0), axis=2)
    slot_ids = jnp.arange(CAP, dtype=jnp.int32)
    hit = want[:, None, :] & (rank[:, None, :] == slot_ids[None, :, None])
    owner = jnp.max(jnp.where(hit, wanted_by[:, None, :], 0), axis=2) - 1
    leaf_of_slot = jnp.max(jnp.where(hit, leaf_ids, 0), axis=2)
    ids = jnp.arange(leaf_count, dtype=jnp.int32) * shares + lax.axis_index("sub")
    ids = (ids[:, None] * node_dev + jnp.arange(node_dev, dtype=jnp.int32)).reshape(-1)
    count = jnp.sum((far_node[:, :, None] == ids).astype(jnp.int32), axis=1)
    return owner, leaf_of_slot, count


def shards(points, charges, near_leaf, far_node, skel_index, skel_weight):
    leaf_count, shares = lax.axis_size("leaf"), lax.axis_size("sub")
    node_dev = skel_index.shape[0]
    owner, leaf_of_slot, count = plan(near_leaf, far_node, node_dev, leaf_count, shares)
    return fused(
        owner, count, leaf_of_slot, points, charges, skel_index, skel_weight, leaf_count, shares
    )


def solution(mesh):
    in_specs = (
        P("leaf", None, "sub"),
        P("leaf", None, "sub"),
        P("leaf", None),
        P("leaf", None),
        P(("leaf", "sub"), None),
        P(("leaf", "sub"), None, None),
    )
    out_specs = P("leaf", None, "sub")
    return jax.shard_map(shards, mesh=mesh, in_specs=in_specs, out_specs=out_specs, check_vma=False)
```

```python
import functools
import math

import jax
import jax.numpy as jnp
from jax import lax
from jax.experimental import pallas as pl
from jax.experimental.pallas import tpu as pltpu
from jax.sharding import PartitionSpec as P

CAP = 3
RATE_SCALE = 2.5
ROWS = 80
PREP = 4
SLOT_UNROLL = 7
MESH = pl.DeviceIdType.MESH


def split3(x):
    a = x.astype(jnp.bfloat16).astype(jnp.float32)
    b = (x - a).astype(jnp.bfloat16).astype(jnp.float32)
    return a, b, (x - a) - b


def stack_rows(main, first, second):
    rows, width = 16, main.shape[1]
    row_id = lax.broadcasted_iota(jnp.int32, (rows, width), 0)
    extra = jnp.zeros((rows, width), jnp.float32)
    for k, piece in enumerate(tuple(first) + tuple(second)):
        extra = jnp.where(row_id == k, piece, extra)
    pad = jnp.zeros((128 - rows - main.shape[0], width), jnp.float32)
    return jnp.concatenate([main, extra, pad], axis=0)


def fused_kernel(
    leaf_count, shares, owner_ref, count_ref, slot_ref, points_ref, charge_ref, index_ref,
    weight_ref, out_ref, ask_ref, tgt_ref, near_ref, skel_ref, wide, send_buf, asked, taug, yown, ynear,
    yskel, acc, stage, held, tgt_send, tgt_recv, ask_send, ask_recv, near_send, near_recv,
    skel_send, skel_recv, sum_send, sum_recv
):
    leaf_dev, features, quarter = points_ref.shape
    node_dev, skel_size = index_ref.shape
    coef = -(RATE_SCALE / features) * math.log2(math.e)
    one = jnp.ones((1, 1), jnp.float32)
    me = lax.axis_index("leaf")
    part = lax.axis_index("sub")

    barrier = pltpu.get_barrier_semaphore()

    def flip(o):
        other, bit = part, 1
        while bit < shares:
            if o & bit:
                other = other + bit - 2 * bit * lax.rem(part // bit, 2)
            bit *= 2
        return other

    def greet_leaf(o, carry):
        pl.semaphore_signal(
            barrier, inc=1, device_id={"leaf": lax.rem(me + o, leaf_count)}, device_id_type=MESH
        )
        return carry

    def greet_sub(o, carry):
        pl.semaphore_signal(
            barrier, inc=1, device_id={"sub": lax.rem(part + o, shares)}, device_id_type=MESH
        )
        return carry

    def fill_ask(k, carry):
        for c in range(CAP):
            ask_ref[k, c : c + 1, :] = jnp.full((1, 128), slot_ref[k, c], jnp.int32)
        ask_ref[k, CAP:, :] = jnp.zeros((8 - CAP, 128), jnp.int32)
        return carry

    lax.fori_loop(1, leaf_count, greet_leaf, 0)
    lax.fori_loop(1, shares, greet_sub, 0)
    lax.fori_loop(0, leaf_count, fill_ask, 0)
    pl.semaphore_wait(barrier, leaf_count + shares - 2)

    def target_copy(o):
        return pltpu.make_async_remote_copy(
            src_ref=points_ref, dst_ref=tgt_ref.at[o],
            send_sem=tgt_send.at[o], recv_sem=tgt_recv.at[o],
            device_id={"sub": flip(o)}, device_id_type=MESH,
        )

    def ask_copy(o):
        k = lax.rem(me + o, leaf_count)
        return pltpu.make_async_remote_copy(
            src_ref=ask_ref.at[k], dst_ref=asked.at[o],
            send_sem=ask_send.at[o], recv_sem=ask_recv.at[o],
            device_id={"leaf": k}, device_id_type=MESH,
        )

    def near_copy(o):
        return pltpu.make_async_remote_copy(
            src_ref=send_buf.at[o], dst_ref=near_ref.at[me],
            send_sem=near_send.at[o], recv_sem=near_recv.at[o],
            device_id={"leaf": lax.rem(me + leaf_count - o, leaf_count)}, device_id_type=MESH,
        )

    def skel_copy(o):
        return pltpu.make_async_remote_copy(
            src_ref=skel_ref.at[me], dst_ref=skel_ref.at[me],
            send_sem=skel_send.at[o], recv_sem=skel_recv.at[o],
            device_id={"leaf": lax.rem(me + o, leaf_count)}, device_id_type=MESH,
        )

    def run(low, high, act):
        def step(o, carry):
            act(o)
            return carry

        lax.fori_loop(low, high, step, 0)

    run(1, leaf_count, lambda o: ask_copy(o).start())
    for o in range(shares - 1, 0, -1):
        target_copy(o).start()
    for i in range(node_dev):
        index = index_ref[i : i + 1, :]
        picked = jnp.zeros((features, skel_size), jnp.float32)
        spot = lax.broadcasted_iota(jnp.int32, (quarter, skel_size), 0)
        for j in range(leaf_dev):
            pick = jnp.where(spot + j * quarter == index, 1.0, 0.0).astype(jnp.bfloat16)
            picked += jnp.dot(points_ref[j], pick, preferred_element_type=jnp.float32)
        skel_ref[me, i] = jnp.concatenate(
            [picked, weight_ref[i].astype(jnp.float32),
             jnp.zeros((ROWS - features - 8, skel_size), jnp.float32)], axis=0
        ).astype(jnp.bfloat16)
    run(1, leaf_count, lambda o: skel_copy(o).start())

    for j in range(leaf_dev):
        wide[j] = jnp.concatenate(
            [points_ref[j].astype(jnp.float32), charge_ref[j].astype(jnp.float32),
             jnp.zeros((ROWS - features - 8, quarter), jnp.float32)], axis=0
        )


    def pack(o):
        ask_copy(o).wait_recv()
        for c in range(CAP):
            row = asked[o, c : c + 1, :]
            block = wide[0]
            for j in range(1, leaf_dev):
                block = jnp.where(row == j, wide[j], block)
            send_buf[o, c] = block.astype(jnp.bfloat16)
        near_copy(o).start()

    run(1, leaf_count, pack)

    def source_rows(block):
        rows = block.astype(jnp.float32)
        sq = split3(jnp.sum(rows * rows, axis=0, keepdims=True))
        return stack_rows(rows, (one, one, one), sq)

    def prep_targets(o, l, block):
        rows = block.astype(jnp.float32)
        sq = split3(jnp.sum(rows * rows, axis=0, keepdims=True))
        taug[l, :, o * quarter : (o + 1) * quarter] = stack_rows(
            -2.0 * rows, sq, (one, one, one)
        ).astype(jnp.bfloat16)

    def prep_own(l, carry):
        yown[l] = source_rows(points_ref[l]).T.astype(jnp.bfloat16)
        prep_targets(0, l, points_ref[l])
        return carry

    lax.fori_loop(0, leaf_dev, prep_own, 0, unroll=PREP)
    half = shares * quarter // 2

    def item_half(l, h, sources, weights):
        dist = jnp.dot(
            sources, taug[l, :, h * half : (h + 1) * half], preferred_element_type=jnp.float32
        )
        kern = jnp.exp2(coef * dist)
        high = kern.astype(jnp.bfloat16)
        low = (kern - high.astype(jnp.float32)).astype(jnp.bfloat16)
        return jnp.dot(weights, high, preferred_element_type=jnp.float32) + jnp.dot(
            weights, low, preferred_element_type=jnp.float32
        )

    def item(l, sources, weights):
        return jnp.concatenate([item_half(l, h, sources, weights) for h in range(2)], axis=1)

    def prep_skel(k, i):
        for h in range(skel_size // 128):
            block = skel_ref[k, i, :features, h * 128 : (h + 1) * 128]
            yskel[h * 128 : (h + 1) * 128] = source_rows(block).T.astype(jnp.bfloat16)
        return skel_ref[k, i, features : features + 8]

    for h in range(2):
        fresh = range(max(1, h * shares // 2), (h + 1) * shares // 2)
        for o in fresh:
            target_copy(o).wait_recv()

        def prep_part(l, carry):
            for o in fresh:
                prep_targets(o, l, tgt_ref[o, l])
            return carry

        def own_step(l, carry):
            acc[l, :, h * half : (h + 1) * half] = item_half(l, h, yown[l], charge_ref[l])
            return carry

        lax.fori_loop(0, leaf_dev, prep_part, 0, unroll=PREP)
        lax.fori_loop(0, leaf_dev, own_step, 0, unroll=leaf_dev)
        for i in range(node_dev):
            weights = prep_skel(me, i)
            for l in range(leaf_dev):
                times = count_ref[l, me * node_dev + i].astype(jnp.float32)
                acc[l, :, h * half : (h + 1) * half] += times * item_half(
                    l, h, yskel[...], weights
                )

    def far_step(o, carry):
        skel_copy(o).wait_recv()
        k = lax.rem(me + leaf_count - o, leaf_count)
        for i in range(node_dev):
            weights = prep_skel(k, i)
            for l in range(leaf_dev):
                times = count_ref[l, k * node_dev + i].astype(jnp.float32)
                acc[l] += times * item(l, yskel[...], weights)
        return carry

    lax.fori_loop(1, leaf_count, far_step, 0)

    run(1, leaf_count, lambda o: near_copy(o).wait_recv())

    def prep_near(o, carry):
        k = lax.rem(me + o, leaf_count)
        for c in range(CAP):
            ynear[o, c] = source_rows(near_ref[k, c, :features]).T.astype(jnp.bfloat16)
        return carry

    lax.fori_loop(1, leaf_count, prep_near, 0)

    def near_step(o, carry):
        k = lax.rem(me + o, leaf_count)
        found = []
        for c in range(CAP):
            owner = owner_ref[k, c]
            value = item(
                jnp.maximum(owner, 0), ynear[o, c], near_ref[k, c, features : features + 8]
            )
            found.append((owner, value))
        for l in range(leaf_dev):
            add = jnp.zeros_like(found[0][1])
            for owner, value in found:
                add += jnp.where(owner == l, value, 0.0)
            acc[l] += add
        return carry

    lax.fori_loop(1, leaf_count, near_step, 0, unroll=SLOT_UNROLL)

    def sum_copy(o):
        return pltpu.make_async_remote_copy(
            src_ref=stage.at[o], dst_ref=held.at[o],
            send_sem=sum_send.at[o], recv_sem=sum_recv.at[o],
            device_id={"sub": flip(o)}, device_id_type=MESH,
        )

    for o in range(1, shares):
        stage[o] = acc[:, :, o * quarter : (o + 1) * quarter]
        sum_copy(o).start()
    run(1, leaf_count, lambda o: ask_copy(o).wait_send())
    for o in range(1, shares):
        target_copy(o).wait_send()
    run(1, leaf_count, lambda o: skel_copy(o).wait_send())
    run(1, leaf_count, lambda o: near_copy(o).wait_send())
    total = acc[:, :, :quarter]
    for o in range(1, shares):
        sum_copy(o).wait_recv()
        total += held[o]
    out_ref[...] = total
    for o in range(1, shares):
        sum_copy(o).wait_send()


def fused(owner, count, slot_leaf, points, charges, skel_index, skel_weight, leaf_count, shares):
    leaf_dev, features, quarter = points.shape
    node_dev, skel_size = skel_index.shape
    vmem = pl.BlockSpec(memory_space=pltpu.VMEM)
    smem = pl.BlockSpec(memory_space=pltpu.SMEM)
    dma = pltpu.SemaphoreType.DMA
    bf16, f32 = jnp.bfloat16, jnp.float32
    return pl.pallas_call(
        functools.partial(fused_kernel, leaf_count, shares),
        out_shape=jax.ShapeDtypeStruct((leaf_dev, 8, quarter), f32),
        in_specs=[smem] * 3 + [vmem] * 4,
        out_specs=vmem,
        scratch_shapes=[
            pltpu.VMEM((leaf_count, 8, 128), jnp.int32),
            pltpu.VMEM((shares, leaf_dev, features, quarter), bf16),
            pltpu.VMEM((leaf_count, CAP, ROWS, quarter), bf16),
            pltpu.VMEM((leaf_count, node_dev, ROWS, skel_size), bf16),
            pltpu.VMEM((leaf_dev, ROWS, quarter), f32),
            pltpu.VMEM((leaf_count, CAP, ROWS, quarter), bf16),
            pltpu.VMEM((leaf_count, 8, 128), jnp.int32),
            pltpu.VMEM((leaf_dev, 128, shares * quarter), bf16),
            pltpu.VMEM((leaf_dev, quarter, 128), bf16),
            pltpu.VMEM((leaf_count, CAP, quarter, 128), bf16),
            pltpu.VMEM((skel_size, 128), bf16),
            pltpu.VMEM((leaf_dev, 8, shares * quarter), f32),
            pltpu.VMEM((shares, leaf_dev, 8, quarter), f32),
            pltpu.VMEM((shares, leaf_dev, 8, quarter), f32),
            dma((shares,)), dma((shares,)),
            dma((leaf_count,)), dma((leaf_count,)),
            dma((leaf_count,)), dma((leaf_count,)),
            dma((leaf_count,)), dma((leaf_count,)),
            dma((shares,)), dma((shares,)),
        ],
        compiler_params=pltpu.CompilerParams(
            collective_id=0, has_side_effects=True, vmem_limit_bytes=56 * 1024 * 1024
        ),
    )(owner, count, slot_leaf, points, charges, skel_index, skel_weight)


def plan(near_leaf, far_node, node_dev, leaf_count, shares):
    leaf_dev = near_leaf.shape[0]
    own_index = lax.axis_index("leaf")
    all_ids = jnp.arange(leaf_count * leaf_dev, dtype=jnp.int32)
    leaf_ids = jnp.arange(leaf_dev, dtype=jnp.int32)
    marks = jnp.where(near_leaf[:, :, None] == all_ids, leaf_ids[:, None, None] + 1, 0)
    wanted_by = jnp.max(marks, axis=(0, 1)).reshape(leaf_count, leaf_dev)
    other = jnp.arange(leaf_count, dtype=jnp.int32)[:, None] != own_index
    wanted_by = jnp.where(other, wanted_by, 0)
    want = wanted_by > 0
    before = leaf_ids[:, None] > leaf_ids[None, :]
    rank = jnp.sum(jnp.where(before[None] & want[:, None, :], 1, 0), axis=2)
    slot_ids = jnp.arange(CAP, dtype=jnp.int32)
    hit = want[:, None, :] & (rank[:, None, :] == slot_ids[None, :, None])
    owner = jnp.max(jnp.where(hit, wanted_by[:, None, :], 0), axis=2) - 1
    leaf_of_slot = jnp.max(jnp.where(hit, leaf_ids, 0), axis=2)
    ids = jnp.arange(leaf_count, dtype=jnp.int32) * shares + lax.axis_index("sub")
    ids = (ids[:, None] * node_dev + jnp.arange(node_dev, dtype=jnp.int32)).reshape(-1)
    count = jnp.sum((far_node[:, :, None] == ids).astype(jnp.int32), axis=1)
    return owner, leaf_of_slot, count


def shards(points, charges, near_leaf, far_node, skel_index, skel_weight):
    leaf_count, shares = lax.axis_size("leaf"), lax.axis_size("sub")
    node_dev = skel_index.shape[0]
    owner, leaf_of_slot, count = plan(near_leaf, far_node, node_dev, leaf_count, shares)
    return fused(
        owner, count, leaf_of_slot, points, charges, skel_index, skel_weight, leaf_count, shares
    )


def solution(mesh):
    in_specs = (
        P("leaf", None, "sub"),
        P("leaf", None, "sub"),
        P("leaf", None),
        P("leaf", None),
        P(("leaf", "sub"), None),
        P(("leaf", "sub"), None, None),
    )
    out_specs = P("leaf", None, "sub")
    return jax.shard_map(shards, mesh=mesh, in_specs=in_specs, out_specs=out_specs, check_vma=False)
```
